32 devices in a mesh: groups: 2 (over y), tm: 16 (over z, x, core).
Axes of the slice: x: 2, y: 2, z: 4, core: 2. Of those that a mesh axis runs over, the one named last changes fastest.
Arguments:
- start_frames: float32 [6, 4, 8, 256], P('groups'), parts along dimension 0, may hold values from -6 to 6
- plan: int32 [32], P(('groups', 'tm')), parts along dimension 0, may hold values from 0 to 999
- noise: float32 [16, 6, 4, 8, 256], P('tm', 'groups'), parts along dimension 1, may hold values from -6 to 6
- w_lift: float32 [3, 128], replicated, may hold values from -3.5 to 3.5
- w_time: float32 [128, 128], replicated, may hold values from -0.75 to 0.75
- spatial: float32 [2, 128, 9], replicated, may hold values from -2 to 2
- temporal: float32 [2, 128, 3], replicated, may hold values from -3.5 to 3.5
- w_point: bfloat16 [2, 128, 128], replicated, may hold values from -0.5 to 0.5
- w_out: float32 [128, 3], replicated, may hold values from -0.5 to 0.5
Outputs:
- trajectory: float32 [16, 6, 4, 8, 256], P('tm', 'groups'), parts along dimension 1
The draws below stay inside these ranges and needn't reach their ends.
There are 2 independent parts, one for each index of `groups`. The reference program is written for one: setup_inputs(seed, part) draws one part's arguments, and reference() takes and returns one part's arrays. A program takes and returns all parts, laid end to end along the dimension named above; an argument that names none is the same for every part. Nothing has to cross between parts.
All inputs are finite; a program needn't handle non-finite values.
Results may differ from the reference program's by a relative error of at most 0.0023.
Values sent between devices are 32-bit elements; how exact they have to be, the bound alone decides.
A program may use at most 64 MiB of HBM per device.

```python
import math
import jax
import jax.numpy as jnp
from jax import lax

C = 3
HID = 128
F = 4
H = 8
W = 256
ITERS = 2
BLOCKS = 2
TIMES = 16


def touch_ends(entries, key, smallest, high):
    longest = entries.shape.index(max(entries.shape))
    spots = []
    for shift in (0, 1):
        where = [jax.random.randint(jax.random.fold_in(key, axis), (), 0, length) for axis, length in enumerate(entries.shape)]
        where[longest] = (where[longest] + shift) % entries.shape[longest]
        spots.append(tuple(where))
    return entries.at[spots[0]].set(smallest).at[spots[1]].set(high)


def block_scale(own_key, extent, cuts, least, largest):
    def one(position, parts):
        draws = jax.random.uniform(jax.random.fold_in(jax.random.fold_in(own_key, 6), position), (parts,), jnp.float32, least / len(cuts), largest / len(cuts))
        return jnp.repeat(jnp.exp(draws), extent[position] // parts).reshape((-1,) + (1,) * (len(extent) - position - 1))

    gain = one(*cuts[0])
    for cut in cuts[1:]:
        gain = gain * one(*cut)
    return gain


def normal_values(rng, extent, scale, limit, cuts=(), held_as=jnp.bfloat16):
    values = scale * jax.random.normal(rng, extent, jnp.float32)
    if cuts:
        values = values * block_scale(rng, extent, cuts, -0.22, 0.18)
    return jnp.clip(values, -limit, limit).astype(held_as)


def setup_inputs(seed: int = 0, part: int = 0) -> dict:
    seeds = jax.random.split(jax.random.key(seed), 10)
    part_splits = jax.random.split(jax.random.fold_in(seeds[9], part), 10)
    start_frames = normal_values(part_splits[0], (C, F, H, W), 1.0, 6.0, (), jnp.float32)
    plan = touch_ends(jax.random.randint(part_splits[1], (TIMES,), 0, 1000), jax.random.fold_in(part_splits[1], 1), 0, 999).astype(jnp.int32)
    noise = normal_values(part_splits[2], (TIMES, C, F, H, W), 1.0, 6.0, ((0, 16),), jnp.float32)
    w_lift = normal_values(seeds[3], (C, HID), C ** -0.5, 3.5, (), jnp.float32)
    w_time = normal_values(seeds[4], (HID, HID), (HID // 2) ** -0.5, 0.75, (), jnp.float32)
    spatial = normal_values(seeds[5], (BLOCKS, HID, 9), 9 ** -0.5, 2.0, (), jnp.float32)
    temporal = normal_values(seeds[6], (BLOCKS, HID, 3), 3 ** -0.5, 3.5, (), jnp.float32)
    w_point = normal_values(seeds[7], (BLOCKS, HID, HID), HID ** -0.5, 0.5)
    w_out = normal_values(seeds[8], (HID, C), HID ** -0.5, 0.5, (), jnp.float32)
    return {"start_frames": start_frames, "plan": plan, "noise": noise, "w_lift": w_lift, "w_time": w_time, "spatial": spatial, "temporal": temporal, "w_point": w_point, "w_out": w_out}


noise_scale = 2.0

def embedding(step_index, width):
    half_width = width // 2
    column = jnp.arange(half_width, dtype=jnp.float32)
    freqs = jnp.exp(-math.log(1000.0) * column / half_width)
    angles = step_index.astype(jnp.float32) * freqs
    return jnp.concatenate([jnp.sin(angles), jnp.cos(angles)])

def convolve(values, kernel_space, kernel_time):
    frames, rows, columns = (values.shape[1], values.shape[2], values.shape[3])
    padded = jnp.pad(values, ((0, 0), (0, 0), (1, 1), (1, 1)))
    spatial_sum = jnp.zeros_like(values)
    for row_tap in range(3):
        for col_tap in range(3):
            spatial_sum = spatial_sum + kernel_space[:, 3 * row_tap + col_tap, None, None, None] * padded[:, :, row_tap:row_tap + rows, col_tap:col_tap + columns]
    framed = jnp.pad(spatial_sum, ((0, 0), (1, 1), (0, 0), (0, 0)))
    result = jnp.zeros_like(values)
    for frame_tap in range(3):
        result = result + kernel_time[:, frame_tap, None, None, None] * framed[:, frame_tap:frame_tap + frames]
    return result

def network(states, step_index, w_lift, w_time, spatial, temporal, w_point, w_out):
    width = w_time.shape[0]
    shape_cells = states.shape[1:]
    bias = jnp.dot(embedding(step_index, width), w_time, precision=lax.Precision.HIGHEST)
    flat_states = states.reshape(states.shape[0], -1)
    lifted = jnp.dot(w_lift.T, flat_states, precision=lax.Precision.HIGHEST) + bias[:, None]
    features = lifted.astype(jnp.bfloat16)
    for block in range(spatial.shape[0]):
        mixed = convolve(features.astype(jnp.float32).reshape((width,) + shape_cells), spatial[block], temporal[block]).reshape(width, -1)
        root_mean = jnp.sqrt(lax.optimization_barrier(jnp.mean(mixed * mixed, axis=0, keepdims=True)) + 1e-06)
        normed = jax.nn.silu(mixed / root_mean).astype(jnp.bfloat16)
        update = jnp.dot(w_point[block].T, normed, preferred_element_type=jnp.float32)
        features = (features.astype(jnp.float32) + update).astype(jnp.bfloat16)
    output = jnp.dot(w_out.T, features.astype(jnp.float32), precision=lax.Precision.HIGHEST)
    return output.reshape(states.shape)

def reference(start_frames, plan, noise, w_lift, w_time, spatial, temporal, w_point, w_out):
    step_size = 1.0 / TIMES

    def drift_of(items):
        states, step_index, noise_now = items
        value = network(states, step_index, w_lift, w_time, spatial, temporal, w_point, w_out)
        return step_size * value + noise_scale * math.sqrt(step_size) * noise_now
    states_all = jnp.broadcast_to(start_frames[None], noise.shape)
    result = states_all
    for iteration in range(ITERS):
        drifts = lax.map(drift_of, (states_all, plan, noise))
        running = jnp.cumsum(drifts, axis=0)
        if iteration + 1 < ITERS:
            before = jnp.concatenate([jnp.zeros_like(drifts[:1]), running[:-1]], axis=0)
            states_all = start_frames[None] + before
        else:
            result = start_frames[None] + running
    return result
```

```python
import functools
import math

import jax
import jax.numpy as jnp
from jax import lax
from jax.experimental import pallas as pl
from jax.experimental.pallas import tpu as pltpu
from jax.sharding import PartitionSpec as P

ITERS = 2
NOISE_SCALE = 2.0
MESH = pl.DeviceIdType.MESH
LANES = 128
HALO = 8
TILE_W = 16


def embedding(step_index, width):
    half_width = width // 2
    column = jnp.arange(half_width, dtype=jnp.float32)
    freqs = jnp.exp(-math.log(1000.0) * column / half_width)
    angles = step_index.astype(jnp.float32) * freqs
    return jnp.concatenate([jnp.sin(angles), jnp.cos(angles)])


def split_bf16(value):
    high = value.astype(jnp.bfloat16).astype(jnp.float32)
    return high, value - high


def kernel(
    n, share,
    start_ref, noise_ref, bias_ref, lift_ref, spatial_ref, temporal_ref, point_ref, wout_ref,
    out_ref,
    feat_a, feat_b, cols, lift_w, value, sent, got, sums, before,
    send_sem, recv_sem,
):
    channels, frames, rows, width = start_ref.shape
    hid = point_ref.shape[1]
    blocks = point_ref.shape[0]
    halves = width // LANES
    step_size = 1.0 / n
    me = lax.axis_index("tm")

    barrier = pltpu.get_barrier_semaphore()

    @pl.loop(1, n)
    def _(k):
        pl.semaphore_signal(
            barrier, inc=1, device_id={"tm": lax.rem(me + k, n)}, device_id_type=MESH
        )

    for feat in (feat_a, feat_b):
        zeros = jnp.zeros((frames * rows, HALO, hid), jnp.float32)
        feat[:, 0:HALO, :] = zeros
        feat[:, HALO + width : HALO + width + HALO, :] = zeros
    cols[...] = jnp.zeros_like(cols)
    cols[:, channels : channels + 1, :] = jnp.ones((frames * rows, 1, width), jnp.float32)
    lift_w[...] = jnp.zeros_like(lift_w)
    high, low = split_bf16(lift_ref[...])
    lift_w[0:channels, :] = high
    lift_w[8 : 8 + channels, :] = high
    lift_w[16 : 16 + channels, :] = low
    high, low = split_bf16(bias_ref[...])
    lift_w[channels : channels + 1, :] = high
    lift_w[16 + channels : 17 + channels, :] = low
    owned = frames * halves * rows // share
    for it in range(ITERS):
        if owned < n:
            sent[it, owned:n] = jnp.zeros((n - owned, channels, share, LANES), jnp.float32)

    def one_block(source, target, block):
        mean_w = jnp.full((hid, hid), 1.0 / hid, jnp.bfloat16)

        @pl.loop(0, width // TILE_W)
        def _(tile):
            w0 = pl.multiple_of(tile * TILE_W, TILE_W)
            taps = [spatial_ref[block, k : k + 1, :] for k in range(9)]
            times = [temporal_ref[block, k : k + 1, :] for k in range(3)]
            mixed = [[None] * rows for _ in range(frames)]
            acc = [[None] * rows for _ in range(frames)]
            for row in range(rows + 1):
                if row < rows:
                    for frame in range(frames):
                        at = frame * rows + row
                        cells = [source[at, pl.ds(w0 + HALO - 1 + c, TILE_W), :] for c in range(3)]
                        for tap in range(3):
                            to = row + 1 - tap
                            if 0 <= to < rows:
                                part = (
                                    taps[3 * tap] * cells[0]
                                    + taps[3 * tap + 1] * cells[1]
                                    + taps[3 * tap + 2] * cells[2]
                                )
                                old = acc[frame][to]
                                acc[frame][to] = part if old is None else old + part
                done = row - 1
                if done >= 0:
                    for frame in range(frames):
                        total = times[1] * acc[frame][done]
                        if frame > 0:
                            total = total + times[0] * acc[frame - 1][done]
                        if frame + 1 < frames:
                            total = total + times[2] * acc[frame + 1][done]
                        mixed[frame][done] = total
            flat = jnp.concatenate([m for per_frame in mixed for m in per_frame], axis=0)
            square = (flat * flat).astype(jnp.bfloat16)
            mean = jnp.dot(square, mean_w, preferred_element_type=jnp.float32)
            half = flat * lax.rsqrt(mean + 1e-06) * 0.5
            normed = (half * jnp.tanh(half) + half).astype(jnp.bfloat16)
            update = jnp.dot(normed, point_ref[block], preferred_element_type=jnp.float32)
            for at in range(frames * rows):
                here = pl.ds(w0 + HALO, TILE_W)
                fresh = source[at, here, :] + update[at * TILE_W : (at + 1) * TILE_W]
                target[at, here, :] = fresh.astype(jnp.bfloat16).astype(jnp.float32)

    def network():
        lift_weights = lift_w[...].astype(jnp.bfloat16)

        @pl.loop(0, frames * rows)
        def _(at):
            state = cols[at]
            high, low = split_bf16(state)
            left = jnp.concatenate([high, low, high, jnp.zeros_like(high)], axis=0)
            lifted = lax.dot_general(
                left.astype(jnp.bfloat16), lift_weights, (((0,), (0,)), ((), ())),
                preferred_element_type=jnp.float32,
            )
            feat_a[at, HALO : HALO + width, :] = lifted.astype(jnp.bfloat16).astype(jnp.float32)

        refs = (feat_a, feat_b)
        for block in range(blocks):
            one_block(refs[block % 2], refs[(block + 1) % 2], block)
        last = refs[blocks % 2]
        for at in range(frames * rows):
            frame, row = divmod(at, rows)
            cells = last[at, HALO : HALO + width, :].astype(jnp.bfloat16)
            both = lax.dot_general(
                wout_ref[...], cells, (((1,), (1,)), ((), ())), preferred_element_type=jnp.float32
            )
            result = both[0:8] + both[8:16]
            for channel in range(channels):
                for part in range(halves):
                    value[channel, frame * halves + part, row : row + 1, :] = result[
                        channel : channel + 1, part * LANES : (part + 1) * LANES
                    ]

    def groups(tile):
        size = share if rows % share == 0 else 1
        for first in range(0, rows, size):
            at = tile * rows + first
            yield at // share, at % share, first, size

    def copy_out(it, peer):
        return pltpu.make_async_remote_copy(
            src_ref=sent.at[it, peer], dst_ref=got.at[it, me],
            send_sem=send_sem.at[it, 0, peer], recv_sem=recv_sem.at[it, 0, me],
            device_id={"tm": peer}, device_id_type=MESH,
        )

    def copy_in(it, peer):
        return pltpu.make_async_remote_copy(
            src_ref=sent.at[it, peer], dst_ref=got.at[it, peer],
            send_sem=send_sem.at[it, 0, peer], recv_sem=recv_sem.at[it, 0, peer],
            device_id={"tm": peer}, device_id_type=MESH,
        )

    def back_out(it, peer):
        return pltpu.make_async_remote_copy(
            src_ref=sums.at[it, peer], dst_ref=before.at[it, me],
            send_sem=send_sem.at[it, 1, peer], recv_sem=recv_sem.at[it, 1, me],
            device_id={"tm": peer}, device_id_type=MESH,
        )

    def back_in(it, peer):
        return pltpu.make_async_remote_copy(
            src_ref=sums.at[it, peer], dst_ref=before.at[it, peer],
            send_sem=send_sem.at[it, 1, peer], recv_sem=recv_sem.at[it, 1, peer],
            device_id={"tm": peer}, device_id_type=MESH,
        )

    for it in range(ITERS):
        for channel in range(channels):
            for frame in range(frames):
                for part in range(halves):
                    lanes = slice(part * LANES, (part + 1) * LANES)
                    state = start_ref[channel, frame, :, lanes]
                    tile = frame * halves + part
                    if it > 0:
                        shift = [
                            before[it - 1, owner, channel, slot : slot + size, :]
                            for owner, slot, first, size in groups(tile)
                        ]
                        state = state + jnp.concatenate(shift, axis=0)
                    for row in range(rows):
                        cols[frame * rows + row, channel : channel + 1, lanes] = state[row : row + 1]
        network()
        for channel in range(channels):
            for frame in range(frames):
                for part in range(halves):
                    lanes = slice(part * LANES, (part + 1) * LANES)
                    tile = frame * halves + part
                    drift = (
                        step_size * value[channel, tile]
                        + NOISE_SCALE * math.sqrt(step_size) * noise_ref[channel, frame, :, lanes]
                    )
                    value[channel, tile] = drift
                    for owner, slot, first, size in groups(tile):
                        sent[it, owner, channel, slot : slot + size, :] = drift[first : first + size]
        if it == 0:
            pl.semaphore_wait(barrier, n - 1)

        @pl.loop(1, n)
        def _(k):
            copy_out(it, lax.rem(me + k, n)).start()

        got[it, me] = sent[it, me]

        def advance(peer, running):
            sums[it, peer] = running

            @pl.when(peer != me)
            def _():
                back_out(it, peer).start()
                copy_in(it, peer).wait_recv()

            return running + got[it, peer]

        lax.fori_loop(0, n, advance, jnp.zeros((channels, share, LANES), jnp.float32))
        before[it, me] = sums[it, me]

        @pl.loop(1, n)
        def _(k):
            peer = lax.rem(me + k, n)
            back_in(it, peer).wait_recv()
            copy_out(it, peer).wait_send()
            back_out(it, peer).wait_send()

    it = ITERS - 1
    for channel in range(channels):
        for frame in range(frames):
            for part in range(halves):
                lanes = slice(part * LANES, (part + 1) * LANES)
                tile = frame * halves + part
                shift = jnp.concatenate(
                    [
                        before[it, owner, channel, slot : slot + size, :]
                        for owner, slot, first, size in groups(tile)
                    ],
                    axis=0,
                )
                out_ref[channel, frame, :, lanes] = (
                    start_ref[channel, frame, :, lanes] + shift + value[channel, tile]
                )


def shards(start_frames, plan, noise, w_lift, w_time, spatial, temporal, w_point, w_out):
    n = lax.axis_size("tm")
    channels, frames, rows, width = start_frames.shape
    hid = w_time.shape[0]
    bias = jnp.dot(embedding(plan[0], hid)[None], w_time, precision=lax.Precision.HIGHEST)
    out_high = lax.reduce_precision(w_out.T, 8, 7)
    out_low = w_out.T - out_high
    pad = ((0, 8 - channels), (0, 0))
    wout = jnp.concatenate([jnp.pad(out_high, pad), jnp.pad(out_low, pad)]).astype(jnp.bfloat16)
    tiles = frames * (width // LANES)
    share = -(-tiles * rows // n)
    vmem = pl.BlockSpec(memory_space=pltpu.VMEM)
    exchange = pltpu.VMEM((ITERS, n, channels, share, LANES), jnp.float32)
    features = pltpu.VMEM((frames * rows, width + 2 * HALO, hid), jnp.float32)
    result = pl.pallas_call(
        functools.partial(kernel, n, share),
        out_shape=jax.ShapeDtypeStruct(start_frames.shape, jnp.float32),
        in_specs=[vmem] * 8,
        out_specs=vmem,
        scratch_shapes=[
            features,
            features,
            pltpu.VMEM((frames * rows, 8, width), jnp.float32),
            pltpu.VMEM((32, hid), jnp.float32),
            pltpu.VMEM((channels, tiles, rows, LANES), jnp.float32),
            exchange,
            exchange,
            exchange,
            exchange,
            pltpu.SemaphoreType.DMA((ITERS, 2, n)),
            pltpu.SemaphoreType.DMA((ITERS, 2, n)),
        ],
        compiler_params=pltpu.CompilerParams(
            collective_id=0, has_side_effects=True, vmem_limit_bytes=48 * 2**20
        ),
    )(
        start_frames, noise[0], bias, w_lift,
        spatial.transpose(0, 2, 1), temporal.transpose(0, 2, 1), w_point, wout,
    )
    return result[None]


def solution(mesh):
    in_specs = (
        P("groups", None, None, None),
        P(("groups", "tm")),
        P("tm", "groups", None, None, None),
        P(),
        P(),
        P(),
        P(),
        P(),
        P(),
    )
    out_specs = P("tm", "groups", None, None, None)
    return jax.shard_map(shards, mesh=mesh, in_specs=in_specs, out_specs=out_specs, check_vma=False)
```

```python
import functools
import math

import jax
import jax.numpy as jnp
from jax import lax
from jax.experimental import pallas as pl
from jax.experimental.pallas import tpu as pltpu
from jax.sharding import PartitionSpec as P

ITERS = 2
NOISE_SCALE = 2.0
MESH = pl.DeviceIdType.MESH
LANES = 128
HALO = 8
TILE_W = 32


def embedding(step_index, width):
    half_width = width // 2
    column = jnp.arange(half_width, dtype=jnp.float32)
    freqs = jnp.exp(-math.log(1000.0) * column / half_width)
    angles = step_index.astype(jnp.float32) * freqs
    return jnp.concatenate([jnp.sin(angles), jnp.cos(angles)])


def split_bf16(value):
    high = value.astype(jnp.bfloat16).astype(jnp.float32)
    return high, value - high


def kernel(
    n, share,
    start_ref, noise_ref, bias_ref, lift_ref, spatial_ref, temporal_ref, point_ref, wout_ref,
    out_ref,
    feat_a, feat_b, cols, lift_w, out_w, conv_w, both_w, pending, value, sent, got, sums, before,
    send_sem, recv_sem,
):
    channels, frames, rows, width = start_ref.shape
    hid = point_ref.shape[1]
    blocks = point_ref.shape[0]
    halves = width // LANES
    step_size = 1.0 / n
    me = lax.axis_index("tm")

    barrier = pltpu.get_barrier_semaphore()

    @pl.loop(1, n)
    def _(k):
        pl.semaphore_signal(
            barrier, inc=1, device_id={"tm": lax.rem(me + k, n)}, device_id_type=MESH
        )

    for feat in (feat_a, feat_b):
        zeros = jnp.zeros((frames * rows, HALO, hid), jnp.float32)
        feat[:, 0:HALO, :] = zeros
        feat[:, HALO + width : HALO + width + HALO, :] = zeros
    cols[...] = jnp.zeros_like(cols)
    cols[:, channels : channels + 1, :] = jnp.ones((frames * rows, 1, width), jnp.float32)
    lift_w[...] = jnp.zeros_like(lift_w)
    high, low = split_bf16(lift_ref[...])
    lift_w[0:channels, :] = high
    lift_w[8 : 8 + channels, :] = high
    lift_w[16 : 16 + channels, :] = low
    out_w[...] = jnp.zeros_like(out_w)
    high, low = split_bf16(wout_ref[...])
    out_w[0:channels, :] = high
    out_w[8 : 8 + channels, :] = low
    high, low = split_bf16(bias_ref[...])
    lift_w[channels : channels + 1, :] = high
    lift_w[16 + channels : 17 + channels, :] = low
    owned = frames * halves * rows // share
    for it in range(ITERS):
        if owned < n:
            sent[it, owned:n] = jnp.zeros((n - owned, channels, share, LANES), jnp.float32)

    spot = lax.broadcasted_iota(jnp.int32, (hid, hid), 0)
    diagonal = spot == lax.broadcasted_iota(jnp.int32, (hid, hid), 1)
    nothing = jnp.zeros((hid, hid), jnp.bfloat16)
    both_w[...] = jnp.zeros_like(both_w)
    for out in range(2):
        here = slice(out * hid, (out + 1) * hid)
        both_w[blocks, here, here] = jnp.full((hid, hid), 4.0 / hid, jnp.bfloat16)
        for block in range(blocks):
            both_w[block, here, here] = point_ref[block]
            for near in range(4):
                tap = near - out
                for col in range(3):
                    there = slice((3 * near + col) * hid, (3 * near + col + 1) * hid)
                    if 0 <= tap < 3:
                        k = 3 * tap + col
                        weight = jnp.where(diagonal, spatial_ref[k, block : block + 1, :], 0.0)
                        conv_w[block, there, here] = weight.astype(jnp.bfloat16)
                    else:
                        conv_w[block, there, here] = nothing

    def one_block(source, target, block):
        pairs = rows // 2
        span = pairs * TILE_W

        def convolve(tile):
            w0 = pl.multiple_of(tile * TILE_W, TILE_W)
            empty = jnp.zeros((TILE_W, hid), jnp.bfloat16)
            stacked = []
            for frame in range(frames):
                cells = [[empty] * 3]
                for row in range(rows):
                    at = frame * rows + row
                    cells.append([
                        source[at, pl.ds(w0 + HALO - 1 + c, TILE_W), :].astype(jnp.bfloat16)
                        for c in range(3)
                    ])
                cells.append([empty] * 3)
                for pair in range(pairs):
                    near = [cells[2 * pair + k][c] for k in range(4) for c in range(3)]
                    stacked.append(jnp.concatenate(near, axis=1))
            return jnp.dot(
                jnp.concatenate(stacked, axis=0), conv_w[block], preferred_element_type=jnp.float32
            )

        def finish(tile, conv):
            w0 = pl.multiple_of(tile * TILE_W, TILE_W)
            times = []
            for k in range(3):
                weight = temporal_ref[k, block : block + 1, :]
                times.append(jnp.concatenate([weight, weight], axis=1))
            placed = [conv[frame * span : (frame + 1) * span] for frame in range(frames)]
            mixed = []
            for frame in range(frames):
                total = times[1] * placed[frame]
                if frame > 0:
                    total = total + times[0] * placed[frame - 1]
                if frame + 1 < frames:
                    total = total + times[2] * placed[frame + 1]
                mixed.append(total)
            flat = jnp.concatenate(mixed, axis=0)
            square = (flat * flat).astype(jnp.bfloat16)
            mean = jnp.dot(square, both_w[blocks], preferred_element_type=jnp.float32)
            half = flat * lax.rsqrt(mean + 4e-06)
            normed = (half * jnp.tanh(half) + half).astype(jnp.bfloat16)
            update = jnp.dot(normed, both_w[block], preferred_element_type=jnp.float32)
            here = pl.ds(w0 + HALO, TILE_W)
            for frame in range(frames):
                for row in range(rows):
                    at = frame * rows + row
                    first = frame * span + (row // 2) * TILE_W
                    out = row % 2
                    part = update[first : first + TILE_W, out * hid : (out + 1) * hid]
                    fresh = source[at, here, :] + part
                    target[at, here, :] = fresh.astype(jnp.bfloat16).astype(jnp.float32)

        tiles = width // TILE_W
        pending[...] = convolve(0)

        @pl.loop(1, tiles)
        def _(tile):
            earlier = pending[...]
            pending[...] = convolve(tile)
            finish(tile - 1, earlier)

        finish(tiles - 1, pending[...])

    def network():
        lift_weights = lift_w[...].astype(jnp.bfloat16)

        @pl.loop(0, frames * rows, unroll=4)
        def _(at):
            state = cols[at]
            high, low = split_bf16(state)
            left = jnp.concatenate([high, low, high, jnp.zeros_like(high)], axis=0)
            lifted = lax.dot_general(
                left.astype(jnp.bfloat16), lift_weights, (((0,), (0,)), ((), ())),
                preferred_element_type=jnp.float32,
            )
            feat_a[at, HALO : HALO + width, :] = lifted.astype(jnp.bfloat16).astype(jnp.float32)

        refs = (feat_a, feat_b)
        for block in range(blocks):
            one_block(refs[block % 2], refs[(block + 1) % 2], block)
        last = refs[blocks % 2]
        out_weights = out_w[...].astype(jnp.bfloat16)
        for at in range(frames * rows):
            frame, row = divmod(at, rows)
            cells = last[at, HALO : HALO + width, :].astype(jnp.bfloat16)
            both = lax.dot_general(
                out_weights, cells, (((1,), (1,)), ((), ())), preferred_element_type=jnp.float32
            )
            result = both[0:8] + both[8:16]
            for channel in range(channels):
                for part in range(halves):
                    value[channel, frame * halves + part, row : row + 1, :] = result[
                        channel : channel + 1, part * LANES : (part + 1) * LANES
                    ]

    def groups(tile):
        size = share if rows % share == 0 else 1
        for first in range(0, rows, size):
            at = tile * rows + first
            yield at // share, at % share, first, size

    def copy_out(it, peer):
        return pltpu.make_async_remote_copy(
            src_ref=sent.at[it, peer], dst_ref=got.at[it, me],
            send_sem=send_sem.at[it, 0, peer], recv_sem=recv_sem.at[it, 0, me],
            device_id={"tm": peer}, device_id_type=MESH,
        )

    def copy_in(it, peer):
        return pltpu.make_async_remote_copy(
            src_ref=sent.at[it, peer], dst_ref=got.at[it, peer],
            send_sem=send_sem.at[it, 0, peer], recv_sem=recv_sem.at[it, 0, peer],
            device_id={"tm": peer}, device_id_type=MESH,
        )

    def back_out(it, peer):
        return pltpu.make_async_remote_copy(
            src_ref=sums.at[it, peer], dst_ref=before.at[it, me],
            send_sem=send_sem.at[it, 1, peer], recv_sem=recv_sem.at[it, 1, me],
            device_id={"tm": peer}, device_id_type=MESH,
        )

    def back_in(it, peer):
        return pltpu.make_async_remote_copy(
            src_ref=sums.at[it, peer], dst_ref=before.at[it, peer],
            send_sem=send_sem.at[it, 1, peer], recv_sem=recv_sem.at[it, 1, peer],
            device_id={"tm": peer}, device_id_type=MESH,
        )

    for it in range(ITERS):
        for channel in range(channels):
            for frame in range(frames):
                for part in range(halves):
                    lanes = slice(part * LANES, (part + 1) * LANES)
                    state = start_ref[channel, frame, :, lanes]
                    tile = frame * halves + part
                    if it > 0:
                        shift = [
                            before[it - 1, owner, channel, slot : slot + size, :]
                            for owner, slot, first, size in groups(tile)
                        ]
                        state = state + jnp.concatenate(shift, axis=0)
                    for row in range(rows):
                        cols[frame * rows + row, channel : channel + 1, lanes] = state[row : row + 1]
        network()
        for channel in range(channels):
            for frame in range(frames):
                for part in range(halves):
                    lanes = slice(part * LANES, (part + 1) * LANES)
                    tile = frame * halves + part
                    drift = (
                        step_size * value[channel, tile]
                        + NOISE_SCALE * math.sqrt(step_size) * noise_ref[channel, frame, :, lanes]
                    )
                    value[channel, tile] = drift
                    for owner, slot, first, size in groups(tile):
                        sent[it, owner, channel, slot : slot + size, :] = drift[first : first + size]
        if it == 0:
            pl.semaphore_wait(barrier, n - 1)

        @pl.loop(1, n)
        def _(k):
            copy_out(it, lax.rem(me + k, n)).start()

        got[it, me] = sent[it, me]

        def advance(peer, running):
            sums[it, peer] = running

            @pl.when(peer != me)
            def _():
                back_out(it, peer).start()
                copy_in(it, peer).wait_recv()

            return running + got[it, peer]

        lax.fori_loop(0, n, advance, jnp.zeros((channels, share, LANES), jnp.float32))
        before[it, me] = sums[it, me]

        @pl.loop(1, n)
        def _(k):
            peer = lax.rem(me + k, n)
            back_in(it, peer).wait_recv()
            copy_out(it, peer).wait_send()
            back_out(it, peer).wait_send()

    it = ITERS - 1
    for channel in range(channels):
        for frame in range(frames):
            for part in range(halves):
                lanes = slice(part * LANES, (part + 1) * LANES)
                tile = frame * halves + part
                shift = jnp.concatenate(
                    [
                        before[it, owner, channel, slot : slot + size, :]
                        for owner, slot, first, size in groups(tile)
                    ],
                    axis=0,
                )
                out_ref[channel, frame, :, lanes] = (
                    start_ref[channel, frame, :, lanes] + shift + value[channel, tile]
                )


def shards(start_frames, plan, noise, w_lift, w_time, spatial, temporal, w_point, w_out):
    n = lax.axis_size("tm")
    channels, frames, rows, width = start_frames.shape
    hid = w_time.shape[0]
    blocks = spatial.shape[0]
    bias = jnp.dot(embedding(plan[0], hid)[None], w_time, precision=lax.Precision.HIGHEST)
    tiles = frames * (width // LANES)
    share = -(-tiles * rows // n)
    vmem = pl.BlockSpec(memory_space=pltpu.VMEM)
    exchange = pltpu.VMEM((ITERS, n, channels, share, LANES), jnp.float32)
    features = pltpu.VMEM((frames * rows, width + 2 * HALO, hid), jnp.float32)
    result = pl.pallas_call(
        functools.partial(kernel, n, share),
        out_shape=jax.ShapeDtypeStruct(start_frames.shape, jnp.float32),
        in_specs=[vmem] * 8,
        out_specs=vmem,
        scratch_shapes=[
            features,
            features,
            pltpu.VMEM((frames * rows, 8, width), jnp.float32),
            pltpu.VMEM((32, hid), jnp.float32),
            pltpu.VMEM((16, hid), jnp.float32),
            pltpu.VMEM((blocks, 12 * hid, 2 * hid), jnp.bfloat16),
            pltpu.VMEM((blocks + 1, 2 * hid, 2 * hid), jnp.bfloat16),
            pltpu.VMEM((frames * rows // 2 * TILE_W, 2 * hid), jnp.float32),
            pltpu.VMEM((channels, tiles, rows, LANES), jnp.float32),
            exchange,
            exchange,
            exchange,
            exchange,
            pltpu.SemaphoreType.DMA((ITERS, 2, n)),
            pltpu.SemaphoreType.DMA((ITERS, 2, n)),
        ],
        compiler_params=pltpu.CompilerParams(
            collective_id=0, has_side_effects=True, vmem_limit_bytes=48 * 2**20
        ),
    )(
        start_frames, noise[0], bias, w_lift,
        spatial.transpose(2, 0, 1), temporal.transpose(2, 0, 1), w_point, w_out.T,
    )
    return result[None]


def solution(mesh):
    in_specs = (
        P("groups", None, None, None),
        P(("groups", "tm")),
        P("tm", "groups", None, None, None),
        P(),
        P(),
        P(),
        P(),
        P(),
        P(),
    )
    out_specs = P("tm", "groups", None, None, None)
    return jax.shard_map(shards, mesh=mesh, in_specs=in_specs, out_specs=out_specs, check_vma=False)
```

```python
import functools
import math

import jax
import jax.numpy as jnp
from jax import lax
from jax.experimental import pallas as pl
from jax.experimental.pallas import tpu as pltpu
from jax.sharding import PartitionSpec as P

ITERS = 2
NOISE_SCALE = 2.0
MESH = pl.DeviceIdType.MESH
LANES = 128
HALO = 8
TILE_W = 32


def embedding(step_index, width):
    half_width = width // 2
    column = jnp.arange(half_width, dtype=jnp.float32)
    freqs = jnp.exp(-math.log(1000.0) * column / half_width)
    angles = step_index.astype(jnp.float32) * freqs
    return jnp.concatenate([jnp.sin(angles), jnp.cos(angles)])


def split_bf16(value):
    high = value.astype(jnp.bfloat16).astype(jnp.float32)
    return high, value - high


def kernel(
    n, share,
    start_ref, noise_ref, bias_ref, lift_ref, spatial_ref, temporal_ref, point_ref, wout_ref,
    out_ref,
    feat_a, feat_b, cols, lift_w, out_w, conv_w, both_w, pending, value, sent, got, sums, before,
    send_sem, recv_sem,
):
    channels, frames, rows, width = start_ref.shape
    hid = point_ref.shape[1]
    blocks = point_ref.shape[0]
    halves = width // LANES
    step_size = 1.0 / n
    me = lax.axis_index("tm")

    barrier = pltpu.get_barrier_semaphore()

    @pl.loop(1, n)
    def _(k):
        pl.semaphore_signal(
            barrier, inc=1, device_id={"tm": lax.rem(me + k, n)}, device_id_type=MESH
        )

    for feat in (feat_a, feat_b):
        zeros = jnp.zeros((frames * rows, HALO, hid), jnp.float32)
        feat[:, 0:HALO, :] = zeros
        feat[:, HALO + width : HALO + width + HALO, :] = zeros
    cols[...] = jnp.zeros_like(cols)
    cols[:, channels : channels + 1, :] = jnp.ones((frames * rows, 1, width), jnp.float32)
    lift_w[...] = jnp.zeros_like(lift_w)
    high, low = split_bf16(lift_ref[...])
    lift_w[0:channels, :] = high
    lift_w[8 : 8 + channels, :] = high
    lift_w[16 : 16 + channels, :] = low
    out_w[...] = jnp.zeros_like(out_w)
    high, low = split_bf16(wout_ref[...])
    out_w[0:channels, :] = high
    out_w[8 : 8 + channels, :] = low
    high, low = split_bf16(bias_ref[...])
    lift_w[channels : channels + 1, :] = high
    lift_w[16 + channels : 17 + channels, :] = low
    owned = frames * halves * rows // share
    for it in range(ITERS):
        if owned < n:
            sent[it, owned:n] = jnp.zeros((n - owned, channels, share, LANES), jnp.float32)

    spot = lax.broadcasted_iota(jnp.int32, (hid, hid), 0)
    diagonal = spot == lax.broadcasted_iota(jnp.int32, (hid, hid), 1)
    both_w[...] = jnp.zeros_like(both_w)
    for out in range(2):
        here = slice(out * hid, (out + 1) * hid)
        both_w[blocks, here, here] = jnp.full((hid, hid), 4.0 / hid, jnp.bfloat16)
        for block in range(blocks):
            both_w[block, here, here] = point_ref[block]
            for near in range(2):
                tap = near + 1 - out
                for col in range(3):
                    there = slice((3 * near + col) * hid, (3 * near + col + 1) * hid)
                    k = 3 * tap + col
                    weight = jnp.where(diagonal, spatial_ref[k, block : block + 1, :], 0.0)
                    conv_w[block, there, here] = weight.astype(jnp.bfloat16)

    def one_block(source, target, block):
        pairs = rows // 2
        span = pairs * TILE_W

        def convolve(tile):
            w0 = pl.multiple_of(tile * TILE_W, TILE_W)
            stacked = []
            for frame in range(frames):
                for pair in range(pairs):
                    near = [
                        source[
                            frame * rows + 2 * pair + k, pl.ds(w0 + HALO - 1 + c, TILE_W), :
                        ].astype(jnp.bfloat16)
                        for k in range(2)
                        for c in range(3)
                    ]
                    stacked.append(jnp.concatenate(near, axis=1))
            return jnp.dot(
                jnp.concatenate(stacked, axis=0), conv_w[block], preferred_element_type=jnp.float32
            )

        def finish(tile, conv):
            w0 = pl.multiple_of(tile * TILE_W, TILE_W)
            times = []
            for k in range(3):
                weight = temporal_ref[k, block : block + 1, :]
                times.append(jnp.concatenate([weight, weight], axis=1))

            def outer(frame, row, tap):
                parts = [
                    spatial_ref[3 * tap + c, block : block + 1, :]
                    * source[frame * rows + row, pl.ds(w0 + HALO - 1 + c, TILE_W), :]
                    for c in range(3)
                ]
                return parts[0] + parts[1] + parts[2]

            placed = []
            for frame in range(frames):
                for pair in range(pairs):
                    first = frame * span + pair * TILE_W
                    halves = []
                    for out, row, tap in ((0, 2 * pair - 1, 0), (1, 2 * pair + 2, 2)):
                        part = conv[first : first + TILE_W, out * hid : (out + 1) * hid]
                        if 0 <= row < rows:
                            part = part + outer(frame, row, tap)
                        halves.append(part)
                    placed.append(jnp.concatenate(halves, axis=1))
            placed = [
                jnp.concatenate(placed[frame * pairs : (frame + 1) * pairs], axis=0)
                for frame in range(frames)
            ]
            mixed = []
            for frame in range(frames):
                total = times[1] * placed[frame]
                if frame > 0:
                    total = total + times[0] * placed[frame - 1]
                if frame + 1 < frames:
                    total = total + times[2] * placed[frame + 1]
                mixed.append(total)
            flat = jnp.concatenate(mixed, axis=0)
            square = flat * flat
            scale = jnp.concatenate(
                [
                    jnp.broadcast_to(
                        lax.rsqrt(
                            jnp.sum(square[:, out * hid : (out + 1) * hid], axis=1, keepdims=True)
                            * (4.0 / hid)
                            + 4e-06
                        ),
                        (frames * span, hid),
                    )
                    for out in range(2)
                ],
                axis=1,
            )
            half = flat * scale
            normed = (half * jnp.tanh(half) + half).astype(jnp.bfloat16)
            update = jnp.dot(normed, both_w[block], preferred_element_type=jnp.float32)
            here = pl.ds(w0 + HALO, TILE_W)
            for frame in range(frames):
                for row in range(rows):
                    at = frame * rows + row
                    first = frame * span + (row // 2) * TILE_W
                    out = row % 2
                    part = update[first : first + TILE_W, out * hid : (out + 1) * hid]
                    fresh = source[at, here, :] + part
                    target[at, here, :] = fresh.astype(jnp.bfloat16).astype(jnp.float32)

        tiles = width // TILE_W
        pending[...] = convolve(0)

        @pl.loop(1, tiles)
        def _(tile):
            earlier = pending[...]
            pending[...] = convolve(tile)
            finish(tile - 1, earlier)

        finish(tiles - 1, pending[...])

    def network():
        lift_weights = lift_w[...].astype(jnp.bfloat16)

        @pl.loop(0, frames * rows, unroll=4)
        def _(at):
            state = cols[at]
            high, low = split_bf16(state)
            left = jnp.concatenate([high, low, high, jnp.zeros_like(high)], axis=0)
            lifted = lax.dot_general(
                left.astype(jnp.bfloat16), lift_weights, (((0,), (0,)), ((), ())),
                preferred_element_type=jnp.float32,
            )
            feat_a[at, HALO : HALO + width, :] = lifted.astype(jnp.bfloat16).astype(jnp.float32)

        refs = (feat_a, feat_b)
        for block in range(blocks):
            one_block(refs[block % 2], refs[(block + 1) % 2], block)
        last = refs[blocks % 2]
        out_weights = out_w[...].astype(jnp.bfloat16)
        for at in range(frames * rows):
            frame, row = divmod(at, rows)
            cells = last[at, HALO : HALO + width, :].astype(jnp.bfloat16)
            both = lax.dot_general(
                out_weights, cells, (((1,), (1,)), ((), ())), preferred_element_type=jnp.float32
            )
            result = both[0:8] + both[8:16]
            for channel in range(channels):
                for part in range(halves):
                    value[channel, frame * halves + part, row : row + 1, :] = result[
                        channel : channel + 1, part * LANES : (part + 1) * LANES
                    ]

    def groups(tile):
        size = share if rows % share == 0 else 1
        for first in range(0, rows, size):
            at = tile * rows + first
            yield at // share, at % share, first, size

    def copy_out(it, peer):
        return pltpu.make_async_remote_copy(
            src_ref=sent.at[it, peer], dst_ref=got.at[it, me],
            send_sem=send_sem.at[it, 0, peer], recv_sem=recv_sem.at[it, 0, me],
            device_id={"tm": peer}, device_id_type=MESH,
        )

    def copy_in(it, peer):
        return pltpu.make_async_remote_copy(
            src_ref=sent.at[it, peer], dst_ref=got.at[it, peer],
            send_sem=send_sem.at[it, 0, peer], recv_sem=recv_sem.at[it, 0, peer],
            device_id={"tm": peer}, device_id_type=MESH,
        )

    def back_out(it, peer):
        return pltpu.make_async_remote_copy(
            src_ref=sums.at[it, peer], dst_ref=before.at[it, me],
            send_sem=send_sem.at[it, 1, peer], recv_sem=recv_sem.at[it, 1, me],
            device_id={"tm": peer}, device_id_type=MESH,
        )

    def back_in(it, peer):
        return pltpu.make_async_remote_copy(
            src_ref=sums.at[it, peer], dst_ref=before.at[it, peer],
            send_sem=send_sem.at[it, 1, peer], recv_sem=recv_sem.at[it, 1, peer],
            device_id={"tm": peer}, device_id_type=MESH,
        )

    for it in range(ITERS):
        for channel in range(channels):
            for frame in range(frames):
                for part in range(halves):
                    lanes = slice(part * LANES, (part + 1) * LANES)
                    state = start_ref[channel, frame, :, lanes]
                    tile = frame * halves + part
                    if it > 0:
                        shift = [
                            before[it - 1, owner, channel, slot : slot + size, :]
                            for owner, slot, first, size in groups(tile)
                        ]
                        state = state + jnp.concatenate(shift, axis=0)
                    for row in range(rows):
                        cols[frame * rows + row, channel : channel + 1, lanes] = state[row : row + 1]
        network()
        for channel in range(channels):
            for frame in range(frames):
                for part in range(halves):
                    lanes = slice(part * LANES, (part + 1) * LANES)
                    tile = frame * halves + part
                    drift = (
                        step_size * value[channel, tile]
                        + NOISE_SCALE * math.sqrt(step_size) * noise_ref[channel, frame, :, lanes]
                    )
                    value[channel, tile] = drift
                    for owner, slot, first, size in groups(tile):
                        sent[it, owner, channel, slot : slot + size, :] = drift[first : first + size]
        if it == 0:
            pl.semaphore_wait(barrier, n - 1)

        @pl.loop(1, n)
        def _(k):
            copy_out(it, lax.rem(me + k, n)).start()

        got[it, me] = sent[it, me]

        def advance(peer, running):
            sums[it, peer] = running

            @pl.when(peer != me)
            def _():
                back_out(it, peer).start()
                copy_in(it, peer).wait_recv()

            return running + got[it, peer]

        lax.fori_loop(0, n, advance, jnp.zeros((channels, share, LANES), jnp.float32))
        before[it, me] = sums[it, me]

        @pl.loop(1, n)
        def _(k):
            peer = lax.rem(me + k, n)
            back_in(it, peer).wait_recv()
            copy_out(it, peer).wait_send()
            back_out(it, peer).wait_send()

    it = ITERS - 1
    for channel in range(channels):
        for frame in range(frames):
            for part in range(halves):
                lanes = slice(part * LANES, (part + 1) * LANES)
                tile = frame * halves + part
                shift = jnp.concatenate(
                    [
                        before[it, owner, channel, slot : slot + size, :]
                        for owner, slot, first, size in groups(tile)
                    ],
                    axis=0,
                )
                out_ref[channel, frame, :, lanes] = (
                    start_ref[channel, frame, :, lanes] + shift + value[channel, tile]
                )


def shards(start_frames, plan, noise, w_lift, w_time, spatial, temporal, w_point, w_out):
    n = lax.axis_size("tm")
    channels, frames, rows, width = start_frames.shape
    hid = w_time.shape[0]
    blocks = spatial.shape[0]
    bias = jnp.dot(embedding(plan[0], hid)[None], w_time, precision=lax.Precision.HIGHEST)
    tiles = frames * (width // LANES)
    share = -(-tiles * rows // n)
    vmem = pl.BlockSpec(memory_space=pltpu.VMEM)
    exchange = pltpu.VMEM((ITERS, n, channels, share, LANES), jnp.float32)
    features = pltpu.VMEM((frames * rows, width + 2 * HALO, hid), jnp.float32)
    result = pl.pallas_call(
        functools.partial(kernel, n, share),
        out_shape=jax.ShapeDtypeStruct(start_frames.shape, jnp.float32),
        in_specs=[vmem] * 8,
        out_specs=vmem,
        scratch_shapes=[
            features,
            features,
            pltpu.VMEM((frames * rows, 8, width), jnp.float32),
            pltpu.VMEM((32, hid), jnp.float32),
            pltpu.VMEM((16, hid), jnp.float32),
            pltpu.VMEM((blocks, 6 * hid, 2 * hid), jnp.bfloat16),
            pltpu.VMEM((blocks + 1, 2 * hid, 2 * hid), jnp.bfloat16),
            pltpu.VMEM((frames * rows // 2 * TILE_W, 2 * hid), jnp.float32),
            pltpu.VMEM((channels, tiles, rows, LANES), jnp.float32),
            exchange,
            exchange,
            exchange,
            exchange,
            pltpu.SemaphoreType.DMA((ITERS, 2, n)),
            pltpu.SemaphoreType.DMA((ITERS, 2, n)),
        ],
        compiler_params=pltpu.CompilerParams(
            collective_id=0, has_side_effects=True, vmem_limit_bytes=48 * 2**20
        ),
    )(
        start_frames, noise[0], bias, w_lift,
        spatial.transpose(2, 0, 1), temporal.transpose(2, 0, 1), w_point, w_out.T,
    )
    return result[None]


def solution(mesh):
    in_specs = (
        P("groups", None, None, None),
        P(("groups", "tm")),
        P("tm", "groups", None, None, None),
        P(),
        P(),
        P(),
        P(),
        P(),
        P(),
    )
    out_specs = P("tm", "groups", None, None, None)
    return jax.shard_map(shards, mesh=mesh, in_specs=in_specs, out_specs=out_specs, check_vma=False)
```
